32 devices in a mesh: context: 2 (over core), fheads: 4 (over y, x), seqs: 4 (over z).
Axes of the slice: x: 2, y: 2, z: 4, core: 2. Of those that a mesh axis runs over, the one named last changes fastest.
Arguments:
- query_rows: bfloat16 [4096, 3072], P(('seqs', 'context'), 'fheads'), parts along dimension 0, may hold values from -5 to 5
- key_rows: bfloat16 [4096, 3072], P(('seqs', 'context'), 'fheads'), parts along dimension 0, may hold values from -5 to 5
- value_rows: bfloat16 [4096, 3072], P(('seqs', 'context'), 'fheads'), parts along dimension 0, may hold values from -10 to 10
- step_sizes: float32 [4096, 4], P(('seqs', 'context'), 'fheads'), parts along dimension 0, may hold values from 2e-05 to 0.0018
- w_gate: bfloat16 [4, 768, 768], P('fheads', 'context'), may hold values from -4 to 4
- w_up: bfloat16 [4, 768, 768], P('fheads', 'context'), may hold values from -4 to 4
- w_down: bfloat16 [4, 768, 768], P('fheads', 'context'), may hold values from -4 to 4
Outputs:
- window_out: bfloat16 [4096, 3072], P(('seqs', 'context'), 'fheads'), parts along dimension 0
- fast_out: bfloat16 [4096, 3072], P(('seqs', 'context'), 'fheads'), parts along dimension 0
The draws below stay inside these ranges and needn't reach their ends.
There are 4 independent parts, one for each index of `seqs`. The reference program is written for one: setup_inputs(seed, part) draws one part's arguments, and reference() takes and returns one part's arrays. A program takes and returns all parts, laid end to end along the dimension named above; an argument that names none is the same for every part. Nothing has to cross between parts.
All inputs are finite; a program needn't handle non-finite values.
Results may differ from the reference program's by a relative error of at most 0.035.
Values may be sent and summed in bfloat16 or wider, within the bound.
No kernel may reach another device: no remote copies, remote signals or barrier semaphores. Data moves between devices by JAX's collectives and lax.ppermute only.
A program may use at most 128 MiB of HBM per device.

```python
import math
import jax
import jax.numpy as jnp
from jax import lax

D = 3072
HEADS = 24
HD = 128
FHEADS = 4
FD = 768
WINDOW = 512
TOK_DEV = 512
LENGTH = 1024
N_CONTEXT = 2


def paired_fields(base):
    first_key = jax.random.fold_in(base, 11)
    second_key = jax.random.fold_in(base, 12)
    limit_value = 5.0 / 1.5
    queries = 1.5 * jax.random.truncated_normal(first_key, -limit_value, limit_value, (LENGTH, D), jnp.float32)
    keys_drawn = 1.5 * jax.random.truncated_normal(second_key, -limit_value, limit_value, (LENGTH, D), jnp.float32)
    return (queries, keys_drawn)


def draw_query_rows(key, part):
    return paired_fields(key)[0].astype(jnp.bfloat16)


def draw_key_rows(key, part):
    return paired_fields(key)[1].astype(jnp.bfloat16)


def draw_step_sizes(key, part):
    position = jnp.arange(LENGTH, dtype=jnp.float32) / max(LENGTH - 1, 1)
    ramp_top = 3.0
    base_rate = jnp.exp(jax.random.uniform(key, (LENGTH, FHEADS), jnp.float32, math.log(2e-05), math.log(0.0002)))
    return base_rate * (ramp_top ** position)[:, None]


def fast_matrix(base, salt, gain):
    salted = jax.random.fold_in(base, salt)
    row_key = jax.random.fold_in(salted, 1)
    column_key = jax.random.fold_in(salted, 2)
    entry_key = jax.random.fold_in(salted, 3)
    spread = 10.0
    ramp_top = 3.0
    ramp = ramp_top ** (jnp.arange(FD, dtype=jnp.float32) / max(FD - 1, 1))
    row_scale = jnp.exp(jax.random.uniform(row_key, (FHEADS, FD, 1), jnp.float32, 0.0, math.log(spread))) * ramp[None, :, None]
    row_scale = row_scale / jnp.sqrt(jnp.sum(row_scale * row_scale, axis=1, keepdims=True))
    column_scale = jnp.exp(jax.random.uniform(column_key, (FHEADS, 1, FD), jnp.float32, 0.0, math.log(spread)))
    column_scale = column_scale / jnp.sqrt(jnp.mean(column_scale * column_scale, axis=2, keepdims=True))
    entries = jax.random.truncated_normal(entry_key, -4.0, 4.0, (FHEADS, FD, FD), jnp.float32)
    return jnp.clip(gain * entries * row_scale * column_scale, -4.0, 4.0)


def draw_w_gate(key, part):
    return fast_matrix(key, 21, 1.0).astype(jnp.bfloat16)


def draw_w_up(key, part):
    return fast_matrix(key, 22, 1.0).astype(jnp.bfloat16)


def draw_w_down(key, part):
    return fast_matrix(key, 23, 2.0).astype(jnp.bfloat16)


def block_scale(rng, shape, split, least, top_value):
    level, own = 1.0, jax.random.fold_in(rng, 6)
    for dim, parts in split:
        heights = jnp.exp(jax.random.uniform(jax.random.fold_in(own, dim), (parts,), jnp.float32, least / len(split), top_value / len(split)))
        level = level * jnp.repeat(heights, shape[dim] // parts).reshape([-1 if axis == dim else 1 for axis in range(len(shape))])
    return level


def scatter_about(key, dims, deviation, limit, pieces=(), held_as=jnp.bfloat16):
    level = block_scale(key, dims, pieces, -0.22, 0.18) if pieces else 1.0
    array = jax.random.normal(key, dims, jnp.float32) * deviation * level
    return jnp.minimum(jnp.maximum(array, -limit), limit).astype(held_as)


def setup_inputs(seed: int = 0, part: int = 0) -> dict:
    key_of = jax.random.split(jax.random.key(seed), 8)
    part_keys = jax.random.split(jax.random.fold_in(key_of[7], part), 8)
    return {
        "query_rows": draw_query_rows(jax.random.fold_in(jax.random.fold_in(key_of[7], part), 71), part),
        "key_rows": draw_key_rows(jax.random.fold_in(jax.random.fold_in(key_of[7], part), 71), part),
        "value_rows": scatter_about(part_keys[2], (LENGTH, D), 2.0, 10.0, ((0, 2), (1, 4))),
        "step_sizes": draw_step_sizes(jax.random.fold_in(jax.random.fold_in(key_of[7], part), 71), part),
        "w_gate": draw_w_gate(jax.random.fold_in(key_of[7], 71), part),
        "w_up": draw_w_up(jax.random.fold_in(key_of[7], 71), part),
        "w_down": draw_w_down(jax.random.fold_in(key_of[7], 71), part),
    }


def unit_rows(values):
    return values * lax.rsqrt(lax.optimization_barrier(jnp.mean(values * values, axis=-1, keepdims=True)) + 1e-06)

def window_block(queries, keys_near, values_near, first_pos):
    row_count = queries.shape[0]
    query_pos = first_pos + jnp.arange(row_count, dtype=jnp.int32)
    key_pos = first_pos - WINDOW + jnp.arange(row_count + WINDOW, dtype=jnp.int32)
    allowed = (key_pos[None, :] >= 0) & (key_pos[None, :] <= query_pos[:, None]) & (key_pos[None, :] > query_pos[:, None] - WINDOW)
    scores = jnp.einsum('ihd,jhd->hij', queries.astype(jnp.float32), keys_near.astype(jnp.float32)) / math.sqrt(HD)
    scores = jnp.where(allowed[None], scores, -1e+30)
    row_max = lax.optimization_barrier(jnp.max(scores, axis=-1, keepdims=True))
    powers = jnp.exp(scores - row_max)
    weights = (powers / lax.optimization_barrier(jnp.sum(powers, axis=-1, keepdims=True))).astype(jnp.bfloat16)
    attended = jnp.einsum('hij,jhd->ihd', weights.astype(jnp.float32), values_near.astype(jnp.float32))
    return attended.astype(jnp.bfloat16)

def attention(query_rows, key_rows, value_rows):
    queries = query_rows.reshape(LENGTH, HEADS, HD)
    padding = jnp.zeros((WINDOW, HEADS, HD), key_rows.dtype)
    keys_padded = jnp.concatenate([padding, key_rows.reshape(LENGTH, HEADS, HD)], axis=0)
    values_padded = jnp.concatenate([padding, value_rows.reshape(LENGTH, HEADS, HD)], axis=0)

    def one_block(block_index):
        first_row = block_index * TOK_DEV
        return window_block(lax.dynamic_slice_in_dim(queries, first_row, TOK_DEV, 0), lax.dynamic_slice_in_dim(keys_padded, first_row, TOK_DEV + WINDOW, 0), lax.dynamic_slice_in_dim(values_padded, first_row, TOK_DEV + WINDOW, 0), first_row)
    blocks = lax.map(one_block, jnp.arange(N_CONTEXT, dtype=jnp.int32))
    return blocks.reshape(LENGTH, HEADS * HD)

def dot_rows(first_op, second_op):
    return lax.dot_general(first_op, second_op, (((0,), (0,)), ((), ())), preferred_element_type=jnp.float32)

def dot_back(first_op, second_op):
    return lax.dot_general(first_op, second_op, (((1,), (1,)), ((), ())), preferred_element_type=jnp.float32)

def renormed(weight, gradient):
    initial = weight.astype(jnp.float32)
    fresh_rows = initial - gradient
    old_ms = lax.optimization_barrier(jnp.mean(initial * initial, axis=0))
    new_ms = lax.optimization_barrier(jnp.mean(fresh_rows * fresh_rows, axis=0))
    return (fresh_rows * jnp.sqrt(old_ms) * lax.rsqrt(new_ms + 1e-06)).astype(jnp.bfloat16)

def apply_fast(fast_queries, gate_w, up_w, down_w):
    gate_new = jnp.dot(fast_queries, gate_w, preferred_element_type=jnp.float32)
    up_new = jnp.dot(fast_queries, up_w, preferred_element_type=jnp.float32)
    hidden_new = (gate_new * jax.nn.sigmoid(gate_new) * up_new).astype(jnp.bfloat16)
    return jnp.dot(hidden_new, down_w, preferred_element_type=jnp.float32).astype(jnp.bfloat16)

def fast_head(queries, keys_in, values_in, step_sizes, gate_w, up_w, down_w):
    fast_keys = unit_rows(keys_in.astype(jnp.float32)).astype(jnp.bfloat16)
    fast_queries = unit_rows(queries.astype(jnp.float32)).astype(jnp.bfloat16)
    target = (-(step_sizes * values_in.astype(jnp.float32))).astype(jnp.bfloat16)
    gate_pre = jnp.dot(fast_keys, gate_w, preferred_element_type=jnp.float32)
    up_pre = jnp.dot(fast_keys, up_w, preferred_element_type=jnp.float32)
    sigmoid_gate = jax.nn.sigmoid(gate_pre)
    hidden = (gate_pre * sigmoid_gate * up_pre).astype(jnp.bfloat16)
    back_grad = dot_back(target, down_w)
    d_gate = (back_grad * up_pre * sigmoid_gate * (1.0 + gate_pre * (1.0 - sigmoid_gate))).astype(jnp.bfloat16)
    d_up = (back_grad * gate_pre * sigmoid_gate).astype(jnp.bfloat16)

    def accumulate(totals, block_index):
        first_row = block_index * TOK_DEV
        keys_block = lax.dynamic_slice_in_dim(fast_keys, first_row, TOK_DEV, 0)
        hidden_block = lax.dynamic_slice_in_dim(hidden, first_row, TOK_DEV, 0)
        target_block = lax.dynamic_slice_in_dim(target, first_row, TOK_DEV, 0)
        gate_block = lax.dynamic_slice_in_dim(d_gate, first_row, TOK_DEV, 0)
        up_block = lax.dynamic_slice_in_dim(d_up, first_row, TOK_DEV, 0)
        partials = (dot_rows(keys_block, gate_block), dot_rows(keys_block, up_block), dot_rows(hidden_block, target_block))
        rounded = tuple((lax.optimization_barrier(term.astype(jnp.bfloat16)).astype(jnp.float32) for term in partials))
        return (tuple((totals[number] + rounded[number] for number in range(3))), None)
    empty = jnp.zeros((FD, FD), jnp.float32)
    sums, _ = lax.scan(accumulate, (empty, empty, empty), jnp.arange(N_CONTEXT, dtype=jnp.int32))
    updated_gate = renormed(gate_w, sums[0])
    updated_up = renormed(up_w, sums[1])
    updated_down = renormed(down_w, sums[2])
    return apply_fast(fast_queries, updated_gate, updated_up, updated_down)

def reference(query_rows, key_rows, value_rows, step_sizes, w_gate, w_up, w_down):
    window_out = attention(query_rows, key_rows, value_rows)
    outputs = []
    for head_number in range(FHEADS):
        columns = slice(head_number * FD, (head_number + 1) * FD)
        outputs.append(fast_head(query_rows[:, columns], key_rows[:, columns], value_rows[:, columns], step_sizes[:, head_number:head_number + 1], w_gate[head_number], w_up[head_number], w_down[head_number]))
    return (window_out, jnp.concatenate(outputs, axis=1))
```

```python
import math

import jax
import jax.numpy as jnp
from jax import lax
from jax.experimental import pallas as pl
from jax.experimental.pallas import tpu as pltpu
from jax.sharding import PartitionSpec as P

HD = 128
WINDOW = 512


def passed_along(x, axis, by):
    peers = lax.axis_size(axis)
    pairs = [(i, i + by) for i in range(peers) if 0 <= i + by < peers]
    return lax.ppermute(x, axis, pairs)


def unit_rows(values):
    return values * lax.rsqrt(jnp.mean(values * values, axis=-1, keepdims=True) + 1e-06)


def window_block(queries, keys_near, values_near, first_pos):
    row_count = queries.shape[0]
    query_pos = first_pos + jnp.arange(row_count, dtype=jnp.int32)
    key_pos = first_pos - WINDOW + jnp.arange(row_count + WINDOW, dtype=jnp.int32)
    allowed = (
        (key_pos[None, :] >= 0)
        & (key_pos[None, :] <= query_pos[:, None])
        & (key_pos[None, :] > query_pos[:, None] - WINDOW)
    )
    scores = jnp.einsum(
        "ihd,jhd->hij", queries, keys_near, preferred_element_type=jnp.float32
    ) / math.sqrt(HD)
    scores = jnp.where(allowed[None], scores, -1e30)
    row_max = jnp.max(scores, axis=-1, keepdims=True)
    powers = jnp.exp(scores - row_max)
    weights = (powers / jnp.sum(powers, axis=-1, keepdims=True)).astype(jnp.bfloat16)
    attended = jnp.einsum("hij,jhd->ihd", weights, values_near, preferred_element_type=jnp.float32)
    return attended.astype(jnp.bfloat16)


def dot_rows(first_op, second_op):
    return lax.dot_general(
        first_op, second_op, (((0,), (0,)), ((), ())), preferred_element_type=jnp.float32
    )


def dot_back(first_op, second_op):
    return lax.dot_general(
        first_op, second_op, (((1,), (1,)), ((), ())), preferred_element_type=jnp.float32
    )


def renormed(weight, gradient):
    initial = weight.astype(jnp.float32)
    fresh_rows = initial - gradient
    old_ms = jnp.mean(initial * initial, axis=0)
    new_ms = jnp.mean(fresh_rows * fresh_rows, axis=0)
    return (fresh_rows * jnp.sqrt(old_ms) * lax.rsqrt(new_ms + 1e-06)).astype(jnp.bfloat16)


def apply_fast(fast_queries, gate_w, up_w, down_w):
    gate_new = jnp.dot(fast_queries, gate_w, preferred_element_type=jnp.float32)
    up_new = jnp.dot(fast_queries, up_w, preferred_element_type=jnp.float32)
    hidden_new = (gate_new * jax.nn.sigmoid(gate_new) * up_new).astype(jnp.bfloat16)
    return jnp.dot(hidden_new, down_w, preferred_element_type=jnp.float32).astype(jnp.bfloat16)


def ring_body(query_rows, key_rows, value_rows, step_sizes, w_gate, w_up, w_down):
    row_count = query_rows.shape[0]
    heads_here = query_rows.shape[1] // HD
    rim_keys, rim_values = passed_along((key_rows, value_rows), "context", 1)
    first_pos = lax.axis_index("context") * row_count
    keys_near = jnp.concatenate([rim_keys, key_rows], axis=0).reshape(
        row_count + WINDOW, heads_here, HD
    )
    values_near = jnp.concatenate([rim_values, value_rows], axis=0).reshape(
        row_count + WINDOW, heads_here, HD
    )
    window_out = window_block(
        query_rows.reshape(row_count, heads_here, HD), keys_near, values_near, first_pos
    )
    window_out = window_out.reshape(row_count, heads_here * HD)
    gathered = (
        lax.all_gather(w_gate, "context", axis=1, tiled=True),
        lax.all_gather(w_up, "context", axis=1, tiled=True),
        lax.all_gather(w_down, "context", axis=1, tiled=True),
    )
    gate_w = gathered[0][0]
    up_w = gathered[1][0]
    down_w = gathered[2][0]
    fast_keys = unit_rows(key_rows.astype(jnp.float32)).astype(jnp.bfloat16)
    fast_queries = unit_rows(query_rows.astype(jnp.float32)).astype(jnp.bfloat16)
    target = (-(step_sizes * value_rows.astype(jnp.float32))).astype(jnp.bfloat16)
    gate_pre = jnp.dot(fast_keys, gate_w, preferred_element_type=jnp.float32)
    up_pre = jnp.dot(fast_keys, up_w, preferred_element_type=jnp.float32)
    sigmoid_gate = jax.nn.sigmoid(gate_pre)
    hidden = (gate_pre * sigmoid_gate * up_pre).astype(jnp.bfloat16)
    back_grad = dot_back(target, down_w)
    d_gate = (back_grad * up_pre * sigmoid_gate * (1.0 + gate_pre * (1.0 - sigmoid_gate))).astype(
        jnp.bfloat16
    )
    d_up = (back_grad * gate_pre * sigmoid_gate).astype(jnp.bfloat16)
    grad_gate = dot_rows(fast_keys, d_gate)
    grad_up = dot_rows(fast_keys, d_up)
    grad_down = dot_rows(hidden, target)
    summed = (
        lax.psum(grad_gate.astype(jnp.bfloat16), "context").astype(jnp.float32),
        lax.psum(grad_up.astype(jnp.bfloat16), "context").astype(jnp.float32),
        lax.psum(grad_down.astype(jnp.bfloat16), "context").astype(jnp.float32),
    )
    updated_gate = renormed(gate_w, summed[0])
    updated_up = renormed(up_w, summed[1])
    updated_down = renormed(down_w, summed[2])
    fast_out = apply_fast(fast_queries, updated_gate, updated_up, updated_down)
    return (window_out, fast_out)


TILE = 256
LOWEST = -1e30
EXP_SCALE = math.log2(math.e) / math.sqrt(HD)
VMEM = pl.BlockSpec(memory_space=pltpu.VMEM)


def call(kernel, out_shape, operands, scratch=(), flops=0, transcendentals=0):
    moved = sum(x.size * x.dtype.itemsize for x in operands)
    moved += sum(math.prod(x.shape) * x.dtype.itemsize for x in out_shape)
    return pl.pallas_call(
        kernel,
        out_shape=out_shape,
        in_specs=[VMEM] * len(operands),
        out_specs=[VMEM] * len(out_shape),
        scratch_shapes=scratch,
        compiler_params=pltpu.CompilerParams(vmem_limit_bytes=40 * 2**20),
        cost_estimate=pl.CostEstimate(
            flops=flops, bytes_accessed=moved, transcendentals=transcendentals
        ),
    )(*operands)


def swapped(x):
    return lax.ppermute(x, "context", [(0, 1), (1, 0)])


def dot_f32(first_op, second_op):
    return jnp.dot(first_op, second_op, preferred_element_type=jnp.float32)


def row_scale(rows):
    wide = rows.astype(jnp.float32)
    return lax.rsqrt(jnp.mean(wide * wide, axis=-1, keepdims=True) + 1e-06)


def tile_order():
    row = lax.broadcasted_iota(jnp.int32, (TILE, TILE), 0)
    col = lax.broadcasted_iota(jnp.int32, (TILE, TILE), 1)
    return row, col


def lane_of(values, lane):
    return values[:, lane : lane + 1]


def diag_kernel(q_ref, k_ref, v_ref, o_ref, stats_ref):
    rows, width = q_ref.shape
    heads = width // HD
    row, col = tile_order()
    lane = lax.broadcasted_iota(jnp.int32, (TILE, HD), 1)
    for first in range(0, rows, TILE):
        here = slice(first, first + TILE)
        stats = jnp.zeros((TILE, HD), jnp.float32)
        for head in range(heads):
            cols = slice(head * HD, (head + 1) * HD)
            query = q_ref[here, cols]
            own = jnp.where(row >= col, dot_back(query, k_ref[here, cols]), LOWEST)
            top = jnp.max(own, axis=-1, keepdims=True)
            if first:
                past = dot_back(query, k_ref[:first, cols])
                top = jnp.maximum(top, jnp.max(past, axis=-1, keepdims=True))
            powers = jnp.exp2((own - top) * EXP_SCALE)
            total = jnp.sum(powers, axis=-1, keepdims=True)
            out = dot_f32(powers.astype(jnp.bfloat16), v_ref[here, cols])
            if first:
                powers = jnp.exp2((past - top) * EXP_SCALE)
                total += jnp.sum(powers, axis=-1, keepdims=True)
                out += dot_f32(powers.astype(jnp.bfloat16), v_ref[:first, cols])
            o_ref[here, cols] = out
            stats = jnp.where(lane == head, top, stats)
            stats = jnp.where(lane == heads + head, total, stats)
        stats_ref[here, :] = stats


def update_kernel(
    k_ref, v_ref, step_ref, k_far_ref, v_far_ref, step_far_ref,
    gate_ref, up_ref, down_ref, gate_far_ref, up_far_ref,
    pack_ref, sums_ref, gate_w, up_w, d_gate, d_up, stepped,
):
    half, width = down_ref.shape
    rows = k_ref.shape[0]
    me = lax.axis_index("context")
    mine = pl.ds(pl.multiple_of(me * half, HD), half)
    far = pl.ds(pl.multiple_of((1 - me) * half, HD), half)
    gate_w[mine, :] = gate_ref[:, mine]
    gate_w[far, :] = gate_far_ref[:, mine]
    up_w[mine, :] = up_ref[:, mine]
    up_w[far, :] = up_far_ref[:, mine]
    blocks = ((k_ref, v_ref, step_ref), (k_far_ref, v_far_ref, step_far_ref))
    for number, (keys, values, steps) in enumerate(blocks):
        for first in range(0, rows, TILE):
            here = slice(first, first + TILE)
            there = slice(number * rows + first, number * rows + first + TILE)
            scale = row_scale(keys[here, :])
            rate = -steps[here, :]
            gate_pre = dot_f32(keys[here, :], gate_w[...]) * scale
            up_pre = dot_f32(keys[here, :], up_w[...]) * scale
            back = dot_back(values[here, :], down_ref[...]) * (rate * scale)
            sigmoid_gate = jax.nn.sigmoid(gate_pre)
            silu = gate_pre * sigmoid_gate
            stepped[there, :] = (silu * up_pre * rate).astype(jnp.bfloat16)
            d_up[there, :] = (back * silu).astype(jnp.bfloat16)
            d_gate[there, :] = (
                back * up_pre * (sigmoid_gate + silu * (1.0 - sigmoid_gate))
            ).astype(jnp.bfloat16)

    def summed(left, right):
        return dot_rows(left[0], right[0]) + dot_rows(left[1], right[1])

    def parts_of(ref):
        return ref[:rows, :], ref[rows:, :]

    both_keys = (k_ref[...], k_far_ref[...])
    both_values = (v_ref[...], v_far_ref[...])
    for weight, slope, place in ((gate_w, d_gate, 0), (up_w, d_up, half)):
        initial = weight[...].astype(jnp.float32)
        fresh = initial - summed(both_keys, parts_of(slope))
        old_ms = jnp.mean(initial * initial, axis=0, keepdims=True)
        new_ms = jnp.mean(fresh * fresh, axis=0, keepdims=True)
        updated = fresh * (jnp.sqrt(old_ms) * lax.rsqrt(new_ms + 1e-06))
        pack_ref[:width, place : place + half] = updated.astype(jnp.bfloat16)
    initial = down_ref[...].astype(jnp.float32)
    fresh = initial - summed(parts_of(stepped), both_values)
    pack_ref[width:, :] = fresh.astype(jnp.bfloat16)
    sums_ref[0:1, :] = jnp.sum(initial * initial, axis=0, keepdims=True)
    sums_ref[1:2, :] = jnp.sum(fresh * fresh, axis=0, keepdims=True)


def half_applied(query, pack_ref):
    width = query.shape[1]
    half = pack_ref.shape[0] - width
    pre = dot_f32(query, pack_ref[:width, :]) * row_scale(query)
    gate_new, up_new = pre[:, :half], pre[:, half:]
    hidden = (gate_new * jax.nn.sigmoid(gate_new) * up_new).astype(jnp.bfloat16)
    return dot_f32(hidden, pack_ref[width:, :])


def prior_kernel(q_ref, k_ref, v_ref, o_ref, stats_ref, pack_ref, out_ref, part_ref):
    rows, width = q_ref.shape
    heads = width // HD
    for first in range(0, rows, TILE):
        here = slice(first, first + TILE)
        part_ref[here, :] = half_applied(q_ref[here, :], pack_ref)

    @pl.when(lax.axis_index("context") == 0)
    def _():
        for first in range(0, rows, TILE):
            here = slice(first, first + TILE)
            stats = stats_ref[here, :]
            for head in range(heads):
                cols = slice(head * HD, (head + 1) * HD)
                total = lane_of(stats, heads + head)
                out_ref[here, cols] = (o_ref[here, cols] / total).astype(jnp.bfloat16)

    @pl.when(lax.axis_index("context") > 0)
    def _():
        row, col = tile_order()
        for first in range(0, rows, TILE):
            here = slice(first, first + TILE)
            stats = stats_ref[here, :]
            for head in range(heads):
                cols = slice(head * HD, (head + 1) * HD)
                query = q_ref[here, cols]
                past_top = lane_of(stats, head)
                own = jnp.where(col > row, dot_back(query, k_ref[here, cols]), LOWEST)
                top = jnp.maximum(past_top, jnp.max(own, axis=-1, keepdims=True))
                if first + TILE < rows:
                    rest = dot_back(query, k_ref[first + TILE :, cols])
                    top = jnp.maximum(top, jnp.max(rest, axis=-1, keepdims=True))
                shrink = jnp.exp2((past_top - top) * EXP_SCALE)
                powers = jnp.exp2((own - top) * EXP_SCALE)
                total = lane_of(stats, heads + head) * shrink
                total += jnp.sum(powers, axis=-1, keepdims=True)
                out = o_ref[here, cols] * shrink
                out += dot_f32(powers.astype(jnp.bfloat16), v_ref[here, cols])
                if first + TILE < rows:
                    powers = jnp.exp2((rest - top) * EXP_SCALE)
                    total += jnp.sum(powers, axis=-1, keepdims=True)
                    out += dot_f32(powers.astype(jnp.bfloat16), v_ref[first + TILE :, cols])
                out_ref[here, cols] = (out / total).astype(jnp.bfloat16)


def finish_kernel(q_ref, pack_ref, part_ref, sums_ref, sums_far_ref, out_ref):
    rows, width = q_ref.shape
    sums = (sums_ref[0:2, :] + sums_far_ref[0:2, :]) / width
    scale = jnp.sqrt(sums[0:1, :]) * lax.rsqrt(sums[1:2, :] + 1e-06)
    for first in range(0, rows, TILE):
        here = slice(first, first + TILE)
        whole = part_ref[here, :] + half_applied(q_ref[here, :], pack_ref)
        out_ref[here, :] = (whole * scale).astype(jnp.bfloat16)


def shape_of(shape, dtype=jnp.float32):
    return jax.ShapeDtypeStruct(shape, dtype)


def pair_body(query_rows, key_rows, value_rows, step_sizes, w_gate, w_up, w_down):
    rows, width = query_rows.shape
    half = w_down.shape[1]
    w_gate, w_up, w_down = w_gate[0], w_up[0], w_down[0]
    gate_far, up_far = swapped(w_gate), swapped(w_up)
    keys_far, values_far = swapped(key_rows), swapped(value_rows)
    steps_far = swapped(step_sizes)
    scores = rows * rows * width
    matmul = 2 * rows * width * half
    own_out, stats = call(
        diag_kernel,
        (shape_of((rows, width)), shape_of((rows, HD))),
        (query_rows, key_rows, value_rows),
        flops=3 * scores,
        transcendentals=scores // HD,
    )
    wide = (2 * rows, half)
    pack, sums = call(
        update_kernel,
        (shape_of((width + half, width), jnp.bfloat16), shape_of((8, width))),
        (
            key_rows, value_rows, step_sizes, keys_far, values_far, steps_far,
            w_gate, w_up, w_down, gate_far, up_far,
        ),
        scratch=[pltpu.VMEM((width, half), jnp.bfloat16)] * 2
        + [pltpu.VMEM(wide, jnp.bfloat16)] * 3,
        flops=12 * matmul,
        transcendentals=2 * rows * half,
    )
    pack_far, sums_far = swapped(pack), swapped(sums)
    window_out, part = call(
        prior_kernel,
        (shape_of((rows, width), jnp.bfloat16), shape_of((rows, width))),
        (query_rows, keys_far, values_far, own_out, stats, pack),
        flops=3 * scores + 3 * matmul,
        transcendentals=scores // HD + rows * half,
    )
    (fast_out,) = call(
        finish_kernel,
        (shape_of((rows, width), jnp.bfloat16),),
        (query_rows, pack_far, part, sums, sums_far),
        flops=3 * matmul,
        transcendentals=rows * half,
    )
    return (window_out, fast_out)


def body(*arrays):
    rows = arrays[0].shape[0]
    pair = lax.axis_size("context") == 2 and rows == WINDOW and rows % TILE == 0
    return (pair_body if pair else ring_body)(*arrays)


def solution(mesh):
    in_specs = (
        P(("seqs", "context"), "fheads"),
        P(("seqs", "context"), "fheads"),
        P(("seqs", "context"), "fheads"),
        P(("seqs", "context"), "fheads"),
        P("fheads", "context", None),
        P("fheads", "context", None),
        P("fheads", "context", None),
    )
    out_specs = (P(("seqs", "context"), "fheads"), P(("seqs", "context"), "fheads"))
    return jax.shard_map(body, mesh=mesh, in_specs=in_specs, out_specs=out_specs, check_vma=False)
```

```python
import functools
import math

import jax
import jax.numpy as jnp
from jax import lax
from jax.experimental import pallas as pl
from jax.experimental.pallas import tpu as pltpu
from jax.sharding import PartitionSpec as P

HD = 128
WINDOW = 512


def passed_along(x, axis, by):
    peers = lax.axis_size(axis)
    pairs = [(i, i + by) for i in range(peers) if 0 <= i + by < peers]
    return lax.ppermute(x, axis, pairs)


def unit_rows(values):
    return values * lax.rsqrt(jnp.mean(values * values, axis=-1, keepdims=True) + 1e-06)


def window_block(queries, keys_near, values_near, first_pos):
    row_count = queries.shape[0]
    query_pos = first_pos + jnp.arange(row_count, dtype=jnp.int32)
    key_pos = first_pos - WINDOW + jnp.arange(row_count + WINDOW, dtype=jnp.int32)
    allowed = (
        (key_pos[None, :] >= 0)
        & (key_pos[None, :] <= query_pos[:, None])
        & (key_pos[None, :] > query_pos[:, None] - WINDOW)
    )
    scores = jnp.einsum(
        "ihd,jhd->hij", queries, keys_near, preferred_element_type=jnp.float32
    ) / math.sqrt(HD)
    scores = jnp.where(allowed[None], scores, -1e30)
    row_max = jnp.max(scores, axis=-1, keepdims=True)
    powers = jnp.exp(scores - row_max)
    weights = (powers / jnp.sum(powers, axis=-1, keepdims=True)).astype(jnp.bfloat16)
    attended = jnp.einsum("hij,jhd->ihd", weights, values_near, preferred_element_type=jnp.float32)
    return attended.astype(jnp.bfloat16)


def dot_rows(first_op, second_op):
    return lax.dot_general(
        first_op, second_op, (((0,), (0,)), ((), ())), preferred_element_type=jnp.float32
    )


def dot_back(first_op, second_op):
    return lax.dot_general(
        first_op, second_op, (((1,), (1,)), ((), ())), preferred_element_type=jnp.float32
    )


def renormed(weight, gradient):
    initial = weight.astype(jnp.float32)
    fresh_rows = initial - gradient
    old_ms = jnp.mean(initial * initial, axis=0)
    new_ms = jnp.mean(fresh_rows * fresh_rows, axis=0)
    return (fresh_rows * jnp.sqrt(old_ms) * lax.rsqrt(new_ms + 1e-06)).astype(jnp.bfloat16)


def apply_fast(fast_queries, gate_w, up_w, down_w):
    gate_new = jnp.dot(fast_queries, gate_w, preferred_element_type=jnp.float32)
    up_new = jnp.dot(fast_queries, up_w, preferred_element_type=jnp.float32)
    hidden_new = (gate_new * jax.nn.sigmoid(gate_new) * up_new).astype(jnp.bfloat16)
    return jnp.dot(hidden_new, down_w, preferred_element_type=jnp.float32).astype(jnp.bfloat16)


def ring_body(query_rows, key_rows, value_rows, step_sizes, w_gate, w_up, w_down):
    row_count = query_rows.shape[0]
    heads_here = query_rows.shape[1] // HD
    rim_keys, rim_values = passed_along((key_rows, value_rows), "context", 1)
    first_pos = lax.axis_index("context") * row_count
    keys_near = jnp.concatenate([rim_keys, key_rows], axis=0).reshape(
        row_count + WINDOW, heads_here, HD
    )
    values_near = jnp.concatenate([rim_values, value_rows], axis=0).reshape(
        row_count + WINDOW, heads_here, HD
    )
    window_out = window_block(
        query_rows.reshape(row_count, heads_here, HD), keys_near, values_near, first_pos
    )
    window_out = window_out.reshape(row_count, heads_here * HD)
    gathered = (
        lax.all_gather(w_gate, "context", axis=1, tiled=True),
        lax.all_gather(w_up, "context", axis=1, tiled=True),
        lax.all_gather(w_down, "context", axis=1, tiled=True),
    )
    gate_w = gathered[0][0]
    up_w = gathered[1][0]
    down_w = gathered[2][0]
    fast_keys = unit_rows(key_rows.astype(jnp.float32)).astype(jnp.bfloat16)
    fast_queries = unit_rows(query_rows.astype(jnp.float32)).astype(jnp.bfloat16)
    target = (-(step_sizes * value_rows.astype(jnp.float32))).astype(jnp.bfloat16)
    gate_pre = jnp.dot(fast_keys, gate_w, preferred_element_type=jnp.float32)
    up_pre = jnp.dot(fast_keys, up_w, preferred_element_type=jnp.float32)
    sigmoid_gate = jax.nn.sigmoid(gate_pre)
    hidden = (gate_pre * sigmoid_gate * up_pre).astype(jnp.bfloat16)
    back_grad = dot_back(target, down_w)
    d_gate = (back_grad * up_pre * sigmoid_gate * (1.0 + gate_pre * (1.0 - sigmoid_gate))).astype(
        jnp.bfloat16
    )
    d_up = (back_grad * gate_pre * sigmoid_gate).astype(jnp.bfloat16)
    grad_gate = dot_rows(fast_keys, d_gate)
    grad_up = dot_rows(fast_keys, d_up)
    grad_down = dot_rows(hidden, target)
    summed = (
        lax.psum(grad_gate.astype(jnp.bfloat16), "context").astype(jnp.float32),
        lax.psum(grad_up.astype(jnp.bfloat16), "context").astype(jnp.float32),
        lax.psum(grad_down.astype(jnp.bfloat16), "context").astype(jnp.float32),
    )
    updated_gate = renormed(gate_w, summed[0])
    updated_up = renormed(up_w, summed[1])
    updated_down = renormed(down_w, summed[2])
    fast_out = apply_fast(fast_queries, updated_gate, updated_up, updated_down)
    return (window_out, fast_out)


TILE = 256
LOWEST = -1e30
EXP_SCALE = math.log2(math.e) / math.sqrt(HD)
ON_CHIP = pl.BlockSpec(memory_space=pltpu.VMEM)
FAR_OFF = pl.BlockSpec(memory_space=pltpu.HBM)


def call(kernel, outs, operands, scratch=(), flops=0, transcendentals=0, loaded=(), stored=()):
    moved = sum(x.size * x.dtype.itemsize for x in operands)
    moved += sum(math.prod(x.shape) * x.dtype.itemsize for x in outs)
    operands = [
        pltpu.with_memory_space_constraint(x, pltpu.HBM) if i in loaded else x
        for i, x in enumerate(operands)
    ]
    return pl.pallas_call(
        kernel,
        out_shape=outs,
        in_specs=[FAR_OFF if i in loaded else ON_CHIP for i in range(len(operands))],
        out_specs=[FAR_OFF if i in stored else ON_CHIP for i in range(len(outs))],
        scratch_shapes=scratch,
        compiler_params=pltpu.CompilerParams(vmem_limit_bytes=40 * 2**20),
        cost_estimate=pl.CostEstimate(
            flops=flops, bytes_accessed=moved, transcendentals=transcendentals
        ),
    )(*operands)


def staggered(units, begin, end, depth=1):
    open_units = []
    for unit in units:
        open_units.append((unit, begin(unit)))
        if len(open_units) > depth:
            end(*open_units.pop(0))
    for entry in open_units:
        end(*entry)


def swapped(x):
    return lax.ppermute(x, "context", [(0, 1), (1, 0)])


def dot_f32(first_op, second_op):
    return jnp.dot(first_op, second_op, preferred_element_type=jnp.float32)


def row_scale(rows):
    wide = rows.astype(jnp.float32)
    return lax.rsqrt(jnp.mean(wide * wide, axis=-1, keepdims=True) + 1e-06)


def head_cols(head):
    return slice(head * HD, (head + 1) * HD)


def row_tiles(rows):
    return [slice(first, first + TILE) for first in range(0, rows, TILE)]


def key_query_order(rows):
    key_pos = lax.broadcasted_iota(jnp.int32, (rows, rows), 0)
    query_pos = lax.broadcasted_iota(jnp.int32, (rows, rows), 1)
    return key_pos, query_pos


def half_of(index, half):
    return pl.ds(pl.multiple_of(index * half, HD), half)


def local_kernel(
    q_hbm, k_hbm, v_hbm, gate_hbm, up_hbm, down_hbm,
    q_ref, k_ref, v_ref, gate_ref, up_ref, down_ref, o_ref, stats_ref, sems,
):
    rows, width = q_ref.shape
    half = down_ref.shape[0]
    mine = half_of(lax.axis_index("context"), half)
    copies = [
        pltpu.make_async_copy(source, target, sems.at[number])
        for number, (source, target) in enumerate(
            (
                (q_hbm, q_ref),
                (k_hbm, k_ref),
                (v_hbm, v_ref),
                (gate_hbm.at[:, mine], gate_ref),
                (up_hbm.at[:, mine], up_ref),
                (down_hbm, down_ref),
            )
        )
    ]
    for copy in copies:
        copy.start()
    for copy in copies[:3]:
        copy.wait()
    key_pos, query_pos = key_query_order(rows)
    allowed = key_pos <= query_pos

    def begin(head):
        return dot_back(k_ref[:, head_cols(head)], q_ref[:, head_cols(head)])

    def end(head, scores):
        cols = head_cols(head)
        scores = jnp.where(allowed, scores, LOWEST)
        top = jnp.max(scores, axis=0, keepdims=True)
        powers = jnp.exp2((scores - top) * EXP_SCALE)
        stats_ref[head : head + 1, :] = top
        stats_ref[8 + head : 9 + head, :] = jnp.sum(powers, axis=0, keepdims=True)
        o_ref[cols, :] = dot_rows(v_ref[:, cols], powers.astype(jnp.bfloat16))

    staggered(range(width // HD), begin, end)
    for copy in copies[3:]:
        copy.wait()


def slopes(keys, values, steps, gate_w, up_w, down_w, d_gate, d_up, stepped):
    half = down_w.shape[0]
    across = jnp.transpose(jnp.broadcast_to(-steps[...], (HD, steps.shape[1])))

    def begin(here):
        return (
            dot_f32(keys[here, :], gate_w[...]),
            dot_f32(keys[here, :], up_w[...]),
            dot_back(values[here, :], down_w[...]),
        )

    def end(here, products):
        scale = jnp.broadcast_to(row_scale(keys[here, :]), (TILE, HD))
        rate = across[here, :]
        scale, rate, both = (
            jnp.concatenate([x] * (half // HD), axis=1) for x in (scale, rate, rate * scale)
        )
        gate_pre = products[0] * scale
        up_pre = products[1] * scale
        back = products[2] * both
        sigmoid_gate = jax.nn.sigmoid(gate_pre)
        silu = gate_pre * sigmoid_gate
        stepped[here, :] = (silu * up_pre * rate).astype(jnp.bfloat16)
        d_up[here, :] = (back * silu).astype(jnp.bfloat16)
        d_gate[here, :] = (
            back * up_pre * (sigmoid_gate + silu * (1.0 - sigmoid_gate))
        ).astype(jnp.bfloat16)

    staggered(row_tiles(keys.shape[0]), begin, end)


def near_kernel(
    k_ref, v_ref, step_ref, gate_ref, up_ref, down_ref, gate_far_ref, up_far_ref,
    gate_w, up_w, d_gate, d_up, stepped,
):
    half = down_ref.shape[0]
    me = lax.axis_index("context")
    mine, far = half_of(me, half), half_of(1 - me, half)
    gate_w[mine, :] = gate_ref[...]
    gate_w[far, :] = gate_far_ref[:, mine]
    up_w[mine, :] = up_ref[...]
    up_w[far, :] = up_far_ref[:, mine]
    slopes(k_ref, v_ref, step_ref, gate_w, up_w, down_ref, d_gate, d_up, stepped)


def far_kernel(
    k_ref, v_ref, d_gate, d_up, stepped, k_far_ref, v_far_ref, step_far_ref,
    gate_w, up_w, down_w, pack_ref, sums_ref, d_gate_far, d_up_far, stepped_far,
):
    half, width = down_w.shape
    slopes(
        k_far_ref, v_far_ref, step_far_ref, gate_w, up_w, down_w, d_gate_far, d_up_far, stepped_far
    )
    for weight, near, far, place in (
        (gate_w, d_gate, d_gate_far, 0),
        (up_w, d_up, d_up_far, half),
    ):
        initial = weight[...].astype(jnp.float32)
        old_ms = jnp.mean(initial * initial, axis=0, keepdims=True)
        fresh = initial - (dot_rows(k_ref[...], near[...]) + dot_rows(k_far_ref[...], far[...]))
        new_ms = jnp.mean(fresh * fresh, axis=0, keepdims=True)
        updated = fresh * (jnp.sqrt(old_ms) * lax.rsqrt(new_ms + 1e-06))
        pack_ref[:width, place : place + half] = updated.astype(jnp.bfloat16)
    initial = down_w[...].astype(jnp.float32)
    sums_ref[0:1, :] = jnp.sum(initial * initial, axis=0, keepdims=True)
    fresh = initial - (
        dot_rows(stepped[...], v_ref[...]) + dot_rows(stepped_far[...], v_far_ref[...])
    )
    pack_ref[width:, :] = fresh.astype(jnp.bfloat16)
    sums_ref[1:2, :] = jnp.sum(fresh * fresh, axis=0, keepdims=True)


def half_applied(q_ref, pack_ref, store):
    rows, width = q_ref.shape
    half = pack_ref.shape[0] - width

    def begin(here):
        return dot_f32(q_ref[here, :], pack_ref[:width, :])

    def end(here, pre):
        pre = pre * row_scale(q_ref[here, :])
        gate_new, up_new = pre[:, :half], pre[:, half:]
        hidden = (gate_new * jax.nn.sigmoid(gate_new) * up_new).astype(jnp.bfloat16)
        store(here, dot_f32(hidden, pack_ref[width:, :]))

    staggered(row_tiles(rows), begin, end)


def prior_kernel(q_ref, k_ref, v_ref, o_ref, stats_ref, pack_ref, out_hbm, part_ref, out_ref, sems):
    rows, width = q_ref.shape
    heads = width // HD

    def store(here, part):
        part_ref[here, :] = part

    half_applied(q_ref, pack_ref, store)
    key_pos, query_pos = key_query_order(rows)
    allowed = key_pos > query_pos + jnp.where(lax.axis_index("context") > 0, 0, rows)

    def written(head):
        cols = head_cols(head)
        return pltpu.make_async_copy(out_ref.at[:, cols], out_hbm.at[:, cols], sems.at[head])

    def begin(head):
        return dot_back(k_ref[:, head_cols(head)], q_ref[:, head_cols(head)])

    def end(head, scores):
        cols = head_cols(head)
        past_top = stats_ref[head : head + 1, :]
        scores = jnp.where(allowed, scores, LOWEST)
        top = jnp.maximum(past_top, jnp.max(scores, axis=0, keepdims=True))
        shrink = jnp.exp2((past_top - top) * EXP_SCALE)
        powers = jnp.exp2((scores - top) * EXP_SCALE)
        total = stats_ref[8 + head : 9 + head, :] * shrink
        total += jnp.sum(powers, axis=0, keepdims=True)
        out = o_ref[cols, :] * shrink + dot_rows(v_ref[:, cols], powers.astype(jnp.bfloat16))
        out_ref[:, cols] = jnp.transpose(out * (1.0 / total)).astype(jnp.bfloat16)
        written(head).start()

    staggered(range(heads), begin, end)
    for head in range(heads):
        written(head).wait()


def finish_kernel(q_ref, pack_ref, part_ref, sums_ref, sums_far_ref, out_hbm, out_ref, sems):
    rows, width = q_ref.shape
    sums = (sums_ref[0:2, :] + sums_far_ref[0:2, :]) / width
    scale = jnp.sqrt(sums[0:1, :]) * lax.rsqrt(sums[1:2, :] + 1e-06)
    tiles = row_tiles(rows)

    def written(here):
        return pltpu.make_async_copy(
            out_ref.at[here, :], out_hbm.at[here, :], sems.at[tiles.index(here)]
        )

    def store(here, part):
        out_ref[here, :] = ((part_ref[here, :] + part) * scale).astype(jnp.bfloat16)
        written(here).start()

    half_applied(q_ref, pack_ref, store)
    for here in tiles:
        written(here).wait()


def shape_of(*shape, dtype=jnp.float32):
    return jax.ShapeDtypeStruct(shape, dtype)


def pair_body(query_rows, key_rows, value_rows, step_sizes, w_gate, w_up, w_down):
    rows, width = query_rows.shape
    half = w_down.shape[1]
    w_gate, w_up, w_down = w_gate[0], w_up[0], w_down[0]
    steps = step_sizes.reshape(1, rows)
    gate_far, up_far = swapped(w_gate), swapped(w_up)
    keys_far, values_far = swapped(key_rows), swapped(value_rows)
    steps_far = swapped(steps)
    brief = functools.partial(shape_of, dtype=jnp.bfloat16)
    scores = rows * rows * width
    matmul = 2 * rows * width * half
    queries, keys, values, gate, up, down, own_out, stats = call(
        local_kernel,
        (
            *(brief(rows, width),) * 3, *(brief(half, half),) * 2, brief(half, width),
            shape_of(width, rows), shape_of(16, rows),
        ),
        (query_rows, key_rows, value_rows, w_gate, w_up, w_down),
        scratch=[pltpu.SemaphoreType.DMA((6,))],
        flops=4 * scores,
        transcendentals=scores // HD,
        loaded=range(6),
    )
    gate_w, up_w, d_gate, d_up, stepped = call(
        near_kernel,
        (*(brief(width, half),) * 2, *(brief(rows, half),) * 3),
        (keys, values, steps, gate, up, down, gate_far, up_far),
        flops=3 * matmul,
        transcendentals=rows * half,
    )
    pack, sums = call(
        far_kernel,
        (brief(width + half, width), shape_of(8, width)),
        (
            keys, values, d_gate, d_up, stepped, keys_far, values_far, steps_far,
            gate_w, up_w, down,
        ),
        scratch=[pltpu.VMEM((rows, half), jnp.bfloat16)] * 3,
        flops=9 * matmul,
        transcendentals=rows * half,
    )
    pack_far, sums_far = swapped(pack), swapped(sums)
    window_out, part = call(
        prior_kernel,
        (brief(rows, width), shape_of(rows, width)),
        (queries, keys_far, values_far, own_out, stats, pack),
        scratch=[pltpu.VMEM((rows, width), jnp.bfloat16), pltpu.SemaphoreType.DMA((width // HD,))],
        flops=4 * scores + 3 * matmul,
        transcendentals=scores // HD + rows * half,
        stored=(0,),
    )
    (fast_out,) = call(
        finish_kernel,
        (brief(rows, width),),
        (queries, pack_far, part, sums, sums_far),
        scratch=[pltpu.VMEM((rows, width), jnp.bfloat16), pltpu.SemaphoreType.DMA((rows // TILE,))],
        flops=3 * matmul,
        transcendentals=rows * half,
        stored=(0,),
    )
    return (window_out, fast_out)


def body(*arrays):
    rows = arrays[0].shape[0]
    pair = lax.axis_size("context") == 2 and rows == WINDOW and rows % TILE == 0
    return (pair_body if pair else ring_body)(*arrays)


def solution(mesh):
    in_specs = (
        P(("seqs", "context"), "fheads"),
        P(("seqs", "context"), "fheads"),
        P(("seqs", "context"), "fheads"),
        P(("seqs", "context"), "fheads"),
        P("fheads", "context", None),
        P("fheads", "context", None),
        P("fheads", "context", None),
    )
    out_specs = (P(("seqs", "context"), "fheads"), P(("seqs", "context"), "fheads"))
    return jax.shard_map(body, mesh=mesh, in_specs=in_specs, out_specs=out_specs, check_vma=False)
```

```python
import functools
import math

import jax
import jax.numpy as jnp
from jax import lax
from jax.experimental import pallas as pl
from jax.experimental.pallas import tpu as pltpu
from jax.sharding import PartitionSpec as P


HD = 128
WINDOW = 512


def passed_along(x, axis, by):
    peers = lax.axis_size(axis)
    pairs = [(i, i + by) for i in range(peers) if 0 <= i + by < peers]
    return lax.ppermute(x, axis, pairs)


def unit_rows(values):
    return values * lax.rsqrt(jnp.mean(values * values, axis=-1, keepdims=True) + 1e-06)


def window_block(queries, keys_near, values_near, first_pos):
    row_count = queries.shape[0]
    query_pos = first_pos + jnp.arange(row_count, dtype=jnp.int32)
    key_pos = first_pos - WINDOW + jnp.arange(row_count + WINDOW, dtype=jnp.int32)
    allowed = (
        (key_pos[None, :] >= 0)
        & (key_pos[None, :] <= query_pos[:, None])
        & (key_pos[None, :] > query_pos[:, None] - WINDOW)
    )
    scores = jnp.einsum(
        "ihd,jhd->hij", queries, keys_near, preferred_element_type=jnp.float32
    ) / math.sqrt(HD)
    scores = jnp.where(allowed[None], scores, -1e30)
    row_max = jnp.max(scores, axis=-1, keepdims=True)
    powers = jnp.exp(scores - row_max)
    weights = (powers / jnp.sum(powers, axis=-1, keepdims=True)).astype(jnp.bfloat16)
    attended = jnp.einsum("hij,jhd->ihd", weights, values_near, preferred_element_type=jnp.float32)
    return attended.astype(jnp.bfloat16)


def dot_rows(first_op, second_op):
    return lax.dot_general(
        first_op, second_op, (((0,), (0,)), ((), ())), preferred_element_type=jnp.float32
    )


def dot_back(first_op, second_op):
    return lax.dot_general(
        first_op, second_op, (((1,), (1,)), ((), ())), preferred_element_type=jnp.float32
    )


def renormed(weight, gradient):
    initial = weight.astype(jnp.float32)
    fresh_rows = initial - gradient
    old_ms = jnp.mean(initial * initial, axis=0)
    new_ms = jnp.mean(fresh_rows * fresh_rows, axis=0)
    return (fresh_rows * jnp.sqrt(old_ms) * lax.rsqrt(new_ms + 1e-06)).astype(jnp.bfloat16)


def apply_fast(fast_queries, gate_w, up_w, down_w):
    gate_new = jnp.dot(fast_queries, gate_w, preferred_element_type=jnp.float32)
    up_new = jnp.dot(fast_queries, up_w, preferred_element_type=jnp.float32)
    hidden_new = (gate_new * jax.nn.sigmoid(gate_new) * up_new).astype(jnp.bfloat16)
    return jnp.dot(hidden_new, down_w, preferred_element_type=jnp.float32).astype(jnp.bfloat16)


def ring_body(query_rows, key_rows, value_rows, step_sizes, w_gate, w_up, w_down):
    row_count = query_rows.shape[0]
    heads_here = query_rows.shape[1] // HD
    rim_keys, rim_values = passed_along((key_rows, value_rows), "context", 1)
    first_pos = lax.axis_index("context") * row_count
    keys_near = jnp.concatenate([rim_keys, key_rows], axis=0).reshape(
        row_count + WINDOW, heads_here, HD
    )
    values_near = jnp.concatenate([rim_values, value_rows], axis=0).reshape(
        row_count + WINDOW, heads_here, HD
    )
    window_out = window_block(
        query_rows.reshape(row_count, heads_here, HD), keys_near, values_near, first_pos
    )
    window_out = window_out.reshape(row_count, heads_here * HD)
    gathered = (
        lax.all_gather(w_gate, "context", axis=1, tiled=True),
        lax.all_gather(w_up, "context", axis=1, tiled=True),
        lax.all_gather(w_down, "context", axis=1, tiled=True),
    )
    gate_w = gathered[0][0]
    up_w = gathered[1][0]
    down_w = gathered[2][0]
    fast_keys = unit_rows(key_rows.astype(jnp.float32)).astype(jnp.bfloat16)
    fast_queries = unit_rows(query_rows.astype(jnp.float32)).astype(jnp.bfloat16)
    target = (-(step_sizes * value_rows.astype(jnp.float32))).astype(jnp.bfloat16)
    gate_pre = jnp.dot(fast_keys, gate_w, preferred_element_type=jnp.float32)
    up_pre = jnp.dot(fast_keys, up_w, preferred_element_type=jnp.float32)
    sigmoid_gate = jax.nn.sigmoid(gate_pre)
    hidden = (gate_pre * sigmoid_gate * up_pre).astype(jnp.bfloat16)
    back_grad = dot_back(target, down_w)
    d_gate = (back_grad * up_pre * sigmoid_gate * (1.0 + gate_pre * (1.0 - sigmoid_gate))).astype(
        jnp.bfloat16
    )
    d_up = (back_grad * gate_pre * sigmoid_gate).astype(jnp.bfloat16)
    grad_gate = dot_rows(fast_keys, d_gate)
    grad_up = dot_rows(fast_keys, d_up)
    grad_down = dot_rows(hidden, target)
    summed = (
        lax.psum(grad_gate.astype(jnp.bfloat16), "context").astype(jnp.float32),
        lax.psum(grad_up.astype(jnp.bfloat16), "context").astype(jnp.float32),
        lax.psum(grad_down.astype(jnp.bfloat16), "context").astype(jnp.float32),
    )
    updated_gate = renormed(gate_w, summed[0])
    updated_up = renormed(up_w, summed[1])
    updated_down = renormed(down_w, summed[2])
    fast_out = apply_fast(fast_queries, updated_gate, updated_up, updated_down)
    return (window_out, fast_out)


TILE = 256
LOWEST = -1e30
EXP_SCALE = math.log2(math.e) / math.sqrt(HD)
ON_CHIP = pl.BlockSpec(memory_space=pltpu.VMEM)
FAR_OFF = pl.BlockSpec(memory_space=pltpu.HBM)


def call(kernel, outs, operands, scratch=(), flops=0, transcendentals=0, loaded=(), stored=()):
    moved = sum(x.size * x.dtype.itemsize for x in operands)
    moved += sum(math.prod(x.shape) * x.dtype.itemsize for x in outs)
    operands = [
        pltpu.with_memory_space_constraint(x, pltpu.HBM) if i in loaded else x
        for i, x in enumerate(operands)
    ]
    return pl.pallas_call(
        kernel,
        out_shape=outs,
        in_specs=[FAR_OFF if i in loaded else ON_CHIP for i in range(len(operands))],
        out_specs=[FAR_OFF if i in stored else ON_CHIP for i in range(len(outs))],
        scratch_shapes=scratch,
        compiler_params=pltpu.CompilerParams(vmem_limit_bytes=40 * 2**20),
        cost_estimate=pl.CostEstimate(
            flops=flops, bytes_accessed=moved, transcendentals=transcendentals
        ),
    )(*operands)


def staggered(units, begin, end, depth=1):
    open_units = []
    for unit in units:
        open_units.append((unit, begin(unit)))
        if len(open_units) > depth:
            end(*open_units.pop(0))
    for entry in open_units:
        end(*entry)


def swapped(x):
    return lax.ppermute(x, "context", [(0, 1), (1, 0)])


def dot_f32(first_op, second_op):
    return jnp.dot(first_op, second_op, preferred_element_type=jnp.float32)


def row_scale(rows):
    wide = rows.astype(jnp.float32)
    return lax.rsqrt(jnp.mean(wide * wide, axis=-1, keepdims=True) + 1e-06)


def head_cols(head):
    return slice(head * HD, (head + 1) * HD)


def row_tiles(rows):
    return [slice(first, first + TILE) for first in range(0, rows, TILE)]


def key_query_order():
    key_pos = lax.broadcasted_iota(jnp.int32, (TILE, TILE), 0)
    query_pos = lax.broadcasted_iota(jnp.int32, (TILE, TILE), 1)
    return key_pos, query_pos


def head_units(rows, width):
    return [(head, here) for head in range(width // HD) for here in row_tiles(rows)]


def half_of(index, half):
    return pl.ds(pl.multiple_of(index * half, HD), half)


def local_kernel(
    q_hbm, k_hbm, v_hbm, gate_hbm, up_hbm, down_hbm,
    q_ref, k_ref, v_ref, gate_ref, up_ref, down_ref, o_ref, stats_ref, sems,
):
    rows, width = q_ref.shape
    half = down_ref.shape[0]
    mine = half_of(lax.axis_index("context"), half)
    early, late = slice(0, 2 * HD), slice(2 * HD, width)
    pairs = [
        (source.at[:, cols], target.at[:, cols])
        for cols in (early, late)
        for source, target in ((k_hbm, k_ref), (q_hbm, q_ref), (v_hbm, v_ref))
    ]
    pairs += [
        (gate_hbm.at[:, mine], gate_ref), (up_hbm.at[:, mine], up_ref), (down_hbm, down_ref)
    ]
    copies = [pltpu.make_async_copy(*pair, sems.at[i]) for i, pair in enumerate(pairs)]
    for copy in copies:
        copy.start()
    key_pos, query_pos = key_query_order()

    def begin(unit):
        head, here = unit
        if here.start == 0:
            for copy in {0: copies[:2], 1: copies[2:3], 2: copies[3:6]}.get(head, ()):
                copy.wait()
        cols = head_cols(head)
        return dot_back(k_ref[: here.stop, cols], q_ref[here, cols])

    def end(unit, scores):
        head, here = unit
        cols = head_cols(head)
        own = jnp.where(key_pos <= query_pos, scores[here.start :], LOWEST)
        scores = jnp.concatenate([scores[: here.start], own]) if here.start else own
        top = jnp.max(scores, axis=0, keepdims=True)
        powers = jnp.exp2((scores - top) * EXP_SCALE)
        stats_ref[head : head + 1, here] = top
        stats_ref[8 + head : 9 + head, here] = jnp.sum(powers, axis=0, keepdims=True)
        o_ref[cols, here] = dot_rows(v_ref[: here.stop, cols], powers.astype(jnp.bfloat16))

    staggered(head_units(rows, width), begin, end, depth=2)
    for copy in copies[6:]:
        copy.wait()


def slopes(keys, values, steps, gate_w, up_w, down_w, d_gate, d_up, stepped):
    half = down_w.shape[0]
    across = jnp.transpose(jnp.broadcast_to(-steps[...], (HD, steps.shape[1])))

    def begin(here):
        return (
            dot_f32(keys[here, :], gate_w[...]),
            dot_f32(keys[here, :], up_w[...]),
            dot_back(values[here, :], down_w[...]),
        )

    def end(here, products):
        scale = jnp.broadcast_to(row_scale(keys[here, :]), (TILE, HD))
        rate = across[here, :]
        scale, rate, both = (
            jnp.concatenate([x] * (half // HD), axis=1) for x in (scale, rate, rate * scale)
        )
        gate_pre = products[0] * scale
        up_pre = products[1] * scale
        back = products[2] * both
        sigmoid_gate = jax.nn.sigmoid(gate_pre)
        silu = gate_pre * sigmoid_gate
        stepped[here, :] = (silu * up_pre * rate).astype(jnp.bfloat16)
        d_up[here, :] = (back * silu).astype(jnp.bfloat16)
        d_gate[here, :] = (
            back * up_pre * (sigmoid_gate + silu * (1.0 - sigmoid_gate))
        ).astype(jnp.bfloat16)

    staggered(row_tiles(keys.shape[0]), begin, end)


def near_kernel(
    k_ref, v_ref, step_ref, gate_ref, up_ref, down_ref, gate_far_ref, up_far_ref,
    gate_w, up_w, d_gate, d_up, stepped,
):
    half = down_ref.shape[0]
    me = lax.axis_index("context")
    mine, far = half_of(me, half), half_of(1 - me, half)
    gate_w[mine, :] = gate_ref[...]
    gate_w[far, :] = gate_far_ref[:, mine]
    up_w[mine, :] = up_ref[...]
    up_w[far, :] = up_far_ref[:, mine]
    slopes(k_ref, v_ref, step_ref, gate_w, up_w, down_ref, d_gate, d_up, stepped)


def far_kernel(
    k_ref, v_ref, d_gate, d_up, stepped, k_far_ref, v_far_ref, step_far_ref,
    gate_w, up_w, down_w, pack_ref, sums_ref, d_gate_far, d_up_far, stepped_far,
):
    half, width = down_w.shape
    slopes(
        k_far_ref, v_far_ref, step_far_ref, gate_w, up_w, down_w, d_gate_far, d_up_far, stepped_far
    )
    for weight, near, far, place in (
        (gate_w, d_gate, d_gate_far, 0),
        (up_w, d_up, d_up_far, half),
    ):
        initial = weight[...].astype(jnp.float32)
        old_ms = jnp.mean(initial * initial, axis=0, keepdims=True)
        fresh = initial - (dot_rows(k_ref[...], near[...]) + dot_rows(k_far_ref[...], far[...]))
        new_ms = jnp.mean(fresh * fresh, axis=0, keepdims=True)
        updated = fresh * (jnp.sqrt(old_ms) * lax.rsqrt(new_ms + 1e-06))
        pack_ref[:width, place : place + half] = updated.astype(jnp.bfloat16)
    initial = down_w[...].astype(jnp.float32)
    sums_ref[0:1, :] = jnp.sum(initial * initial, axis=0, keepdims=True)
    fresh = initial - (
        dot_rows(stepped[...], v_ref[...]) + dot_rows(stepped_far[...], v_far_ref[...])
    )
    pack_ref[width:, :] = fresh.astype(jnp.bfloat16)
    sums_ref[1:2, :] = jnp.sum(fresh * fresh, axis=0, keepdims=True)


def half_applied(q_ref, pack_ref, store):
    width = q_ref.shape[1]
    half = pack_ref.shape[0] - width

    def begin(here):
        return dot_f32(q_ref[here, :], pack_ref[:width, :])

    def end(here, pre):
        pre = pre * row_scale(q_ref[here, :])
        gate_new, up_new = pre[:, :half], pre[:, half:]
        hidden = (gate_new * jax.nn.sigmoid(gate_new) * up_new).astype(jnp.bfloat16)
        for first in range(0, width, TILE):
            cols = slice(first, first + TILE)
            store(here, cols, dot_f32(hidden, pack_ref[width:, cols]))

    return begin, end


def prior_kernel(q_ref, k_ref, v_ref, o_ref, stats_ref, pack_ref, out_ref, part_ref):
    rows, width = q_ref.shape

    def store(here, cols, part):
        part_ref[here, cols] = part

    begin_tile, end_tile = half_applied(q_ref, pack_ref, store)
    key_pos, query_pos = key_query_order()
    absent = jnp.where(lax.axis_index("context") > 0, 0.0, -LOWEST)

    def begin(unit):
        if isinstance(unit, slice):
            return begin_tile(unit)
        head, here = unit
        cols = head_cols(head)
        return dot_back(k_ref[here.start :, cols], q_ref[here, cols])

    def end(unit, scores):
        if isinstance(unit, slice):
            return end_tile(unit, scores)
        head, here = unit
        cols = head_cols(head)
        past_top = stats_ref[head : head + 1, here]
        own = jnp.where(key_pos > query_pos, scores[:TILE], LOWEST)
        scores = jnp.concatenate([own, scores[TILE:]]) if here.stop < rows else own
        top = jnp.maximum(past_top, jnp.max(scores, axis=0, keepdims=True) - absent)
        shrink = jnp.exp2((past_top - top) * EXP_SCALE)
        powers = jnp.exp2((scores - (top + absent)) * EXP_SCALE)
        total = stats_ref[8 + head : 9 + head, here] * shrink
        total += jnp.sum(powers, axis=0, keepdims=True)
        out = dot_rows(v_ref[here.start :, cols], powers.astype(jnp.bfloat16))
        out = (o_ref[cols, here] * shrink + out) * (1.0 / total)
        out_ref[here, cols] = jnp.transpose(out).astype(jnp.bfloat16)

    staggered([*row_tiles(rows), *head_units(rows, width)], begin, end, depth=2)


def finish_kernel(
    q_ref, pack_ref, part_ref, sums_ref, sums_far_ref, window_ref, out_hbm, window_hbm, out_ref, sems
):
    rows, width = q_ref.shape
    window_copy = pltpu.make_async_copy(window_ref, window_hbm, sems.at[0])
    window_copy.start()
    sums = (sums_ref[0:2, :] + sums_far_ref[0:2, :]) / width
    scale = jnp.sqrt(sums[0:1, :]) * lax.rsqrt(sums[1:2, :] + 1e-06)
    tiles = row_tiles(rows)
    written = [window_copy]

    def store(here, cols, part):
        out_ref[here, cols] = ((part_ref[here, cols] + part) * scale[:, cols]).astype(jnp.bfloat16)
        copy = pltpu.make_async_copy(
            out_ref.at[here, cols], out_hbm.at[here, cols], sems.at[len(written)]
        )
        copy.start()
        written.append(copy)

    staggered(tiles, *half_applied(q_ref, pack_ref, store))
    for copy in written:
        copy.wait()


def shape_of(*shape, dtype=jnp.float32):
    return jax.ShapeDtypeStruct(shape, dtype)


def pair_body(query_rows, key_rows, value_rows, step_sizes, w_gate, w_up, w_down):
    rows, width = query_rows.shape
    half = w_down.shape[1]
    w_gate, w_up, w_down = w_gate[0], w_up[0], w_down[0]
    steps = step_sizes.reshape(1, rows)
    gate_far, up_far = swapped(w_gate), swapped(w_up)
    keys_far, values_far = swapped(key_rows), swapped(value_rows)
    steps_far = swapped(steps)
    brief = functools.partial(shape_of, dtype=jnp.bfloat16)
    scores = rows * rows * width
    matmul = 2 * rows * width * half
    queries, keys, values, gate, up, down, own_out, stats = call(
        local_kernel,
        (
            *(brief(rows, width),) * 3, *(brief(half, half),) * 2, brief(half, width),
            shape_of(width, rows), shape_of(16, rows),
        ),
        (query_rows, key_rows, value_rows, w_gate, w_up, w_down),
        scratch=[pltpu.SemaphoreType.DMA((9,))],
        flops=4 * scores,
        transcendentals=scores // HD,
        loaded=range(6),
    )
    gate_w, up_w, d_gate, d_up, stepped = call(
        near_kernel,
        (*(brief(width, half),) * 2, *(brief(rows, half),) * 3),
        (keys, values, steps, gate, up, down, gate_far, up_far),
        flops=3 * matmul,
        transcendentals=rows * half,
    )
    pack, sums = call(
        far_kernel,
        (brief(width + half, width), shape_of(8, width)),
        (
            keys, values, d_gate, d_up, stepped, keys_far, values_far, steps_far,
            gate_w, up_w, down,
        ),
        scratch=[pltpu.VMEM((rows, half), jnp.bfloat16)] * 3,
        flops=9 * matmul,
        transcendentals=rows * half,
    )
    pack_far, sums_far = swapped(pack), swapped(sums)
    window, part = call(
        prior_kernel,
        (brief(rows, width), shape_of(rows, width)),
        (queries, keys_far, values_far, own_out, stats, pack),
        flops=4 * scores + 3 * matmul,
        transcendentals=scores // HD + rows * half,
    )
    fast_out, window_out = call(
        finish_kernel,
        (brief(rows, width),) * 2,
        (queries, pack_far, part, sums, sums_far, window),
        scratch=[
            pltpu.VMEM((rows, width), jnp.bfloat16),
            pltpu.SemaphoreType.DMA((1 + rows * width // TILE**2,)),
        ],
        flops=3 * matmul,
        transcendentals=rows * half,
        stored=(0, 1),
    )
    return (window_out, fast_out)


def body(*arrays):
    rows = arrays[0].shape[0]
    pair = lax.axis_size("context") == 2 and rows == WINDOW and rows % TILE == 0
    return (pair_body if pair else ring_body)(*arrays)


def solution(mesh):
    in_specs = (
        P(("seqs", "context"), "fheads"),
        P(("seqs", "context"), "fheads"),
        P(("seqs", "context"), "fheads"),
        P(("seqs", "context"), "fheads"),
        P("fheads", "context", None),
        P("fheads", "context", None),
        P("fheads", "context", None),
    )
    out_specs = (P(("seqs", "context"), "fheads"), P(("seqs", "context"), "fheads"))
    return jax.shard_map(body, mesh=mesh, in_specs=in_specs, out_specs=out_specs, check_vma=False)
```
